32 devices in a mesh: col: 8 (over z, x), row: 4 (over y, core).
Axes of the slice: x: 2, y: 2, z: 4, core: 2. Of those that a mesh axis runs over, the one named last changes fastest.
Arguments:
- weight: float32 [8192, 16384], P('row', 'col'), may hold values from -6 to 6
- momentum: float32 [8192, 16384], P('row', 'col'), may hold values from -6 to 6
- gradient: bfloat16 [8192, 16384], P('row', 'col'), may hold values from -6 to 6
- right_factor: float32 [16384, 256], P('col'), may hold values from -6 to 6
Outputs:
- new_weight: float32 [8192, 16384], P('row', 'col')
- new_momentum: float32 [8192, 16384], P('row', 'col')
- new_factor: float32 [16384, 256], P('col')
The draws below stay inside these ranges and needn't reach their ends.
All inputs are finite; a program needn't handle non-finite values.
Results may differ from the reference program's by a relative error of at most 0.0003.
Values sent between devices are 32-bit elements; how exact they have to be, the bound alone decides.
No kernel may reach another device: no remote copies, remote signals or barrier semaphores. Data moves between devices by JAX's collectives and lax.ppermute only.
A program may use at most 128 MiB of HBM per device.

```python
import jax
import jax.numpy as jnp
from jax import lax

D_IN = 16384
ROWS = 8192
RANK = 256


def steps_of(key, extent, split, low, top_value):
    gain, own = 1.0, jax.random.fold_in(key, 6)
    for dim, blocks in split:
        heights = jnp.exp(jax.random.uniform(jax.random.fold_in(own, dim), (blocks,), jnp.float32, low / len(split), top_value / len(split)))
        gain = gain * jnp.repeat(heights, extent[dim] // blocks).reshape([-1 if axis == dim else 1 for axis in range(len(extent))])
    return gain


def noise(stream_key, extent, scale, most, pieces=(), dtype=jnp.bfloat16):
    result = scale * jax.random.normal(stream_key, extent, jnp.float32)
    if pieces:
        result = result * steps_of(stream_key, extent, pieces, -0.22, 0.18)
    return jnp.clip(result, -most, most).astype(dtype)


def setup_inputs(seed: int = 0) -> dict:
    arg_keys = jax.random.split(jax.random.key(seed), 5)
    weight = noise(arg_keys[0], (ROWS, D_IN), 1.0, 6.0, ((0, 4), (1, 8)), jnp.float32)
    momentum = noise(arg_keys[1], (ROWS, D_IN), 1.0, 6.0, ((0, 4), (1, 8)), jnp.float32)
    gradient = noise(arg_keys[2], (ROWS, D_IN), 1.0, 6.0, ((0, 4), (1, 8)))
    right_factor = noise(arg_keys[3], (D_IN, RANK), 1.0, 6.0, ((0, 8),), jnp.float32)
    return {"weight": weight, "momentum": momentum, "gradient": gradient, "right_factor": right_factor}


def matmul(left_side, right_side):
    return jnp.dot(left_side.astype(jnp.float32), right_side.astype(jnp.float32), precision=lax.Precision.HIGHEST, preferred_element_type=jnp.float32)

def reference(weight, momentum, gradient, right_factor):
    combined = momentum + gradient.astype(jnp.float32)
    left_raw = matmul(combined, right_factor)
    gram_matrix = matmul(left_raw.T, left_raw)
    lower = jnp.linalg.cholesky(gram_matrix)
    left_factor = lax.linalg.triangular_solve(lower, left_raw, left_side=False, lower=True, transpose_a=True)
    right_raw = matmul(combined.T, left_factor)
    new_momentum = combined - 0.05 * matmul(left_factor, right_raw.T)
    squares = lax.optimization_barrier(jnp.sum(right_raw * right_raw, axis=0))
    column_scale = jnp.sqrt(squares / D_IN + 1e-06)
    new_factor = right_raw / column_scale
    new_weight = weight - 0.5 * matmul(left_factor, new_factor.T)
    return (new_weight, new_momentum, new_factor)
```

```python
import functools

import jax
import jax.numpy as jnp
from jax import lax
from jax.experimental import pallas as pl
from jax.experimental.pallas import tpu as pltpu
from jax.sharding import PartitionSpec as P


F32, BF16 = jnp.float32, jnp.bfloat16
HIGHEST = lax.Precision.HIGHEST
NN = (((1,), (0,)), ((), ()))
TN = (((0,), (0,)), ((), ()))
NT = (((1,), (1,)), ((), ()))


def dot(first, second, dims, precision=None):
    return lax.dot_general(first, second, dims, precision=precision, preferred_element_type=F32)


def halves(value):
    high = value.astype(BF16)
    return high, (value - high.astype(F32)).astype(BF16)


def call(kernel, flops, nbytes, limit=16, **kwargs):
    return pl.pallas_call(
        kernel,
        cost_estimate=pl.CostEstimate(flops=flops, bytes_accessed=nbytes, transcendentals=0),
        compiler_params=pltpu.CompilerParams(vmem_limit_bytes=limit << 20),
        **kwargs,
    )


def tile(rows, most=256):
    return min(rows, most)


def fixed(i):
    return (0, 0)


def near_core(value):
    return pltpu.with_memory_space_constraint(value, pltpu.VMEM)


def in_hbm(value):
    return pltpu.with_memory_space_constraint(value, pltpu.HBM)


RESIDENT = pl.BlockSpec(memory_space=pltpu.VMEM)


def along(value, axis):
    high, low = halves(value)
    return jnp.concatenate([high, high, low], axis=axis)


def along_swapped(value, axis):
    high, low = halves(value)
    return jnp.concatenate([high, low, high], axis=axis)


def left_kernel(opening, m_ref, g_ref, r_ref, p_ref, c_ref, *refs):
    i = pl.program_id(0)
    split_ref = refs[0] if opening else r_ref
    if opening:

        @pl.when(i == 0)
        def _():
            split_ref[...] = along_swapped(r_ref[...], 0)

    combined = m_ref[...] + g_ref[...].astype(F32)
    c_ref[...] = combined
    p_ref[...] = dot(along(combined, 1), split_ref[...], NN)


def left_part(momentum, gradient, right, opening, start, rows):
    n = momentum.shape[1]
    rank = right.shape[1]
    bm = tile(rows)
    first = start // bm
    block = pl.BlockSpec((bm, n), lambda i: (i + first, 0))
    here = lambda i: (i, 0)
    out_specs = [pl.BlockSpec((bm, rank), here), pl.BlockSpec((bm, n), here)]
    out_shape = [jax.ShapeDtypeStruct((rows, rank), F32), pltpu.HBM((rows, n), F32)]
    if opening:
        out_specs.append(RESIDENT)
        out_shape.append(pltpu.VMEM((3 * n, rank), BF16))
        right, spec = in_hbm(right), pl.BlockSpec((n, rank), fixed)
    else:
        right, spec = near_core(right), RESIDENT
    return call(
        functools.partial(left_kernel, opening), 6 * rows * n * rank, rows * n * 6,
        grid=(rows // bm,),
        in_specs=[block, block, spec],
        out_specs=tuple(out_specs),
        out_shape=tuple(out_shape),
    )(in_hbm(momentum), in_hbm(gradient), right)


def cross_kernel(l_ref, c_ref, *refs):
    acc = refs[-1]
    n = c_ref.shape[1]
    left = along(l_ref[...].T, 1)
    step = min(n, 512)
    for c in range(0, n, step):
        value = dot(left, along_swapped(c_ref[:, c : c + step], 0), NN)
        acc[:, c : c + step] = value + refs[0][:, c : c + step] if len(refs) > 1 else value


def cross_part(left, combined, before):
    rows, rank = left.shape
    n = combined.shape[1]
    extra = [] if before is None else [before]
    return call(
        cross_kernel, 6 * rows * n * rank, rank * n * 8,
        in_specs=[RESIDENT] * (2 + len(extra)),
        out_specs=RESIDENT,
        out_shape=jax.ShapeDtypeStruct((rank, n), F32),
        input_output_aliases={2: 0} if extra else {},
    )(left, near_core(combined), *extra)


def gram_kernel(*refs):
    left = refs[0][...]
    value = dot(left, left, TN, HIGHEST)
    refs[-1][...] = value + refs[1][...] if len(refs) > 2 else value


def gram_part(left, before):
    rows, rank = left.shape
    extra = [] if before is None else [before]
    return call(
        gram_kernel, 12 * rows * rank * rank, rows * rank * 4,
        out_shape=jax.ShapeDtypeStruct((rank, rank), F32),
    )(left, *extra)


def inverse_kernel(g_ref, x_ref, work):
    rank = g_ref.shape[0]
    b = min(32, rank)
    rows = lax.broadcasted_iota(jnp.int32, (rank, rank), 0)
    cols = lax.broadcasted_iota(jnp.int32, (rank, rank), 1)
    work[:, :rank] = g_ref[...]
    work[:, rank:] = jnp.where(rows == cols, 1.0, 0.0).astype(F32)
    r = lax.broadcasted_iota(jnp.int32, (b, b), 0)
    c = lax.broadcasted_iota(jnp.int32, (b, b), 1)
    for j in range(0, rank, b):
        block = work[j : j + b, j : j + b]
        inv = jnp.where(r == c, 1.0, 0.0).astype(F32)
        aug = jnp.concatenate([block, inv], axis=1)
        sub = lax.broadcasted_iota(jnp.int32, (b, 2 * b), 0)
        pivots = jnp.zeros((b, 1), F32)
        for i in range(b):
            pivot = aug[i : i + 1, i : i + 1]
            row = aug[i : i + 1, :] * (1.0 / pivot)
            col = jnp.where(sub[:, :1] > i, aug[:, i : i + 1], 0.0)
            pivots = jnp.where(sub[:, :1] == i, pivot, pivots)
            aug = aug - col * row
        inv = aug[:, b:] * lax.rsqrt(pivots)
        panel = dot(inv, work[j : j + b, :], NN, HIGHEST)
        work[j : j + b, :] = panel
        if j + b < rank:
            work[j + b :, :] -= dot(panel[:, j + b : rank], panel, TN, HIGHEST)
    x_ref[...] = work[:, rank:]


def inverse_factor(gram):
    rank = gram.shape[0]
    return call(
        inverse_kernel, 12 * rank**3 * 20, rank * rank * 8,
        out_shape=jax.ShapeDtypeStruct((rank, rank), F32),
        scratch_shapes=[pltpu.VMEM((rank, 2 * rank), F32)],
    )(gram)


def basis_kernel(l_ref, x_ref, o_ref):
    o_ref[...] = dot(l_ref[...], x_ref[...], NT, HIGHEST)


def basis(left, inverse):
    rows, rank = left.shape
    return call(
        basis_kernel, 12 * rows * rank * rank, rows * rank * 8,
        out_shape=jax.ShapeDtypeStruct((rows, rank), F32),
    )(left, inverse)


def right_kernel(x_ref, z_ref, o_ref, s_ref):
    value = dot(x_ref[...], z_ref[...], NN, HIGHEST)
    o_ref[...] = value
    s_ref[...] = jnp.broadcast_to(jnp.sum(value * value, axis=1, keepdims=True), s_ref.shape)


def right_side(inverse, cross):
    rank, n = cross.shape
    return call(
        right_kernel, 12 * n * rank * rank, n * rank * 8,
        out_shape=(jax.ShapeDtypeStruct((rank, n), F32), jax.ShapeDtypeStruct((rank, 128), F32)),
    )(inverse, cross)


def momentum_kernel(parts, half_ref, l_ref, r_ref, *refs):
    o_ref, split = refs[-2:]
    i = pl.program_id(0)
    _, width = o_ref.shape

    @pl.when(i == 0)
    def _():
        high, low = halves(r_ref[...])
        split[...] = jnp.concatenate([high, low], axis=0)

    left = l_ref[...].astype(BF16)
    update = dot(jnp.concatenate([left, left], axis=1), split[...], NN)
    columns = pl.ds(pl.multiple_of(half_ref[0] * width, width), width)
    for part in range(parts):

        @pl.when(i == part)
        def _():
            o_ref[...] = refs[part][:, columns] - 0.05 * update


def momentum_half(half, left, right, parts, first, before):
    rows, rank = left.shape
    width = right.shape[1]
    bm = parts[0].shape[0]
    extra = [] if before is None else [before]
    n_in = 3 + len(parts) + len(extra)
    return pl.pallas_call(
        functools.partial(momentum_kernel, len(parts)),
        name="momentum",
        cost_estimate=pl.CostEstimate(flops=4 * bm * len(parts) * width * rank, bytes_accessed=bm * len(parts) * width * 4, transcendentals=0),
        compiler_params=pltpu.CompilerParams(vmem_limit_bytes=16 << 20),
        grid_spec=pltpu.PrefetchScalarGridSpec(
            num_scalar_prefetch=1,
            grid=(len(parts),),
            in_specs=[
                pl.BlockSpec((bm, rank), lambda i, half: (i + first, 0)),
                pl.BlockSpec((rank, width), lambda i, half: (0, 0)),
            ] + [RESIDENT] * len(parts) + [pl.BlockSpec(memory_space=pl.ANY)] * len(extra),
            out_specs=pl.BlockSpec((bm, width), lambda i, half: (i + first, half[0])),
            scratch_shapes=[pltpu.VMEM((2 * rank, width), BF16)],
        ),
        out_shape=jax.ShapeDtypeStruct((rows, 2 * width), F32),
        input_output_aliases={n_in - 1: 0} if extra else {},
    )(half, left, right, *[near_core(part) for part in parts], *extra)


def weight_kernel(count, half_ref, l_ref, a_ref, b_ref, s_ref, w_ref, o_ref, f_ref, split):
    @pl.when(pl.program_id(0) == 0)
    def _():
        scale = jnp.sqrt(s_ref[:, :1] / count + 1e-06)
        width = a_ref.shape[1]
        for side, ref in ((half_ref[0], a_ref), (1 - half_ref[0], b_ref)):
            factor = ref[...] / scale
            start = pl.multiple_of(side * width, width)
            split[:, pl.ds(start, width)] = along_swapped(factor, 0)
            f_ref[pl.ds(start, width), :] = factor.T

    update = dot(along(l_ref[...], 1), split[...], NN)
    o_ref[...] = w_ref[...] - 0.5 * update


def weight_update(half, left, own, other, squares, weight, count):
    rows, n = weight.shape
    rank, width = own.shape
    bm = tile(rows)
    row = lambda i, half: (i, 0)
    still = lambda i, half: (0, 0)
    return pl.pallas_call(
        functools.partial(weight_kernel, float(count)),
        name="weight",
        cost_estimate=pl.CostEstimate(flops=6 * rows * n * rank, bytes_accessed=rows * n * 8, transcendentals=0),
        compiler_params=pltpu.CompilerParams(vmem_limit_bytes=16 << 20),
        grid_spec=pltpu.PrefetchScalarGridSpec(
            num_scalar_prefetch=1,
            grid=(rows // bm,),
            in_specs=[
                pl.BlockSpec((bm, rank), row),
                pl.BlockSpec((rank, width), still),
                pl.BlockSpec((rank, width), still),
                pl.BlockSpec(squares.shape, still),
                pl.BlockSpec((bm, n), row),
            ],
            out_specs=(pl.BlockSpec((bm, n), row), pl.BlockSpec((n, rank), still)),
            scratch_shapes=[pltpu.VMEM((3 * rank, n), BF16)],
        ),
        out_shape=(jax.ShapeDtypeStruct((rows, n), F32), jax.ShapeDtypeStruct((n, rank), F32)),
    )(half, left, own, other, squares, near_core(weight))


class Axis:
    def __init__(self, mesh, name):
        self.name, self.size = name, mesh.shape[name]
        self.bits = self.size.bit_length() - 1

    def swap(self, value, bit):
        return lax.ppermute(value, self.name, [(i, i ^ (1 << bit)) for i in range(self.size)])

    def place(self, bit):
        return (lax.axis_index(self.name) >> bit) & 1

    def exchange(self, value, bit):
        return value + self.swap(value, bit)

    def scatter(self, value, bit, dim=0):
        half = value.shape[dim] // 2
        here = self.place(bit)
        keep = lax.dynamic_slice_in_dim(value, here * half, half, dim)
        return keep + self.swap(lax.dynamic_slice_in_dim(value, (1 - here) * half, half, dim), bit)

    def gather(self, value, bit):
        other = self.swap(value, bit)
        first = jnp.concatenate([value, other])
        return jnp.where(self.place(bit) == 0, first, jnp.concatenate([other, value]))

    def total(self, value, bits):
        for bit in bits[:-1]:
            value = self.scatter(value, bit)
        value = self.exchange(value, bits[-1])
        for bit in bits[-2::-1]:
            value = self.gather(value, bit)
        return value


def on_device(col, row, weight, momentum, gradient, right_factor):
    rows, n = momentum.shape
    count = n * col.size
    near = col.bits // 2
    order = tuple(range(col.bits))
    orders = (order, order[near:] + order[:near] if near == 0 else (near,) + tuple(b for b in order if b != near))
    parts = 4
    size = rows // parts
    lefts, combined, cross, gram, right = [], [], None, None, right_factor
    for part in range(parts):
        got = left_part(momentum, gradient, right, part == 0, part * size, size)
        right = got[2] if part == 0 else right
        combined.append(got[1])
        lefts.append(col.total(got[0], orders[part % 2]))
    for part in range(parts - 1):
        gram = gram_part(lefts[part], gram)
        cross = cross_part(lefts[part], combined[part], cross)
    gram = row.exchange(gram_part(lefts[-1], gram), 0)
    for bit in range(1, row.bits - 1):
        gram = row.exchange(gram, bit)
    last, gram = lax.optimization_barrier((lefts[-1], gram))
    other = row.swap(gram, row.bits - 1)
    cross = cross_part(last, combined[-1], cross)
    gram = gram + other
    half = row.place(0).astype(jnp.int32).reshape(1)
    cross = row.scatter(cross, 0, 1)
    for bit in range(1, row.bits - 1):
        cross = row.exchange(cross, bit)
    other = row.swap(cross, row.bits - 1)
    gram, _ = lax.optimization_barrier((gram, cross))
    inverse = inverse_factor(gram)
    left = basis(jnp.concatenate(lefts), inverse)
    own, squares = right_side(inverse, cross + other)
    other = row.swap(own, 0)
    squares = row.exchange(squares, 0)
    pieces = [(half, own, 0, parts), (1 - half, other, 0, parts // 2), (1 - half, other, parts // 2, parts)]
    new_momentum = None
    for bit in range(col.bits):
        squares = col.exchange(squares, bit)
        if bit < len(pieces):
            side, value, start, stop = pieces[bit]
            new_momentum = momentum_half(side, left, value, combined[start:stop], start, new_momentum)
    new_weight, new_factor = weight_update(half, left, own, other, squares, weight, count)
    return new_weight, new_momentum, new_factor


def solution(mesh):
    col, row = Axis(mesh, "col"), Axis(mesh, "row")

    def body(*args):
        return on_device(col, row, *args)

    in_specs = (P("row", "col"), P("row", "col"), P("row", "col"), P("col", None))
    out_specs = (P("row", "col"), P("row", "col"), P("col", None))
    return jax.shard_map(body, mesh=mesh, in_specs=in_specs, out_specs=out_specs, check_vma=False)
```

```python
import functools

import jax
import jax.numpy as jnp
from jax import lax
from jax.experimental import pallas as pl
from jax.experimental.pallas import tpu as pltpu
from jax.sharding import PartitionSpec as P


F32, BF16 = jnp.float32, jnp.bfloat16
HIGHEST = lax.Precision.HIGHEST
NN = (((1,), (0,)), ((), ()))
TN = (((0,), (0,)), ((), ()))
NT = (((1,), (1,)), ((), ()))


def dot(first, second, dims, precision=None):
    return lax.dot_general(first, second, dims, precision=precision, preferred_element_type=F32)


def halves(value):
    high = value.astype(BF16)
    return high, (value - high.astype(F32)).astype(BF16)


def call(kernel, flops, nbytes, limit=16, **kwargs):
    return pl.pallas_call(
        kernel,
        cost_estimate=pl.CostEstimate(flops=flops, bytes_accessed=nbytes, transcendentals=0),
        compiler_params=pltpu.CompilerParams(vmem_limit_bytes=limit << 20),
        **kwargs,
    )


def tile(rows, most=256):
    return min(rows, most)


def fixed(i):
    return (0, 0)


def near_core(value):
    return pltpu.with_memory_space_constraint(value, pltpu.VMEM)


def in_hbm(value):
    return pltpu.with_memory_space_constraint(value, pltpu.HBM)


RESIDENT = pl.BlockSpec(memory_space=pltpu.VMEM)


def along(value, axis):
    high, low = halves(value)
    return jnp.concatenate([high, high, low], axis=axis)


def along_swapped(value, axis):
    high, low = halves(value)
    return jnp.concatenate([high, low, high], axis=axis)


def left_kernel(opening, m_ref, g_ref, r_ref, p_ref, c_ref, *refs):
    i = pl.program_id(0)
    split_ref = refs[0] if opening else r_ref
    if opening:

        @pl.when(i == 0)
        def _():
            split_ref[...] = along_swapped(r_ref[...], 0)

    combined = m_ref[...] + g_ref[...].astype(F32)
    c_ref[...] = combined
    p_ref[...] = dot(along(combined, 1), split_ref[...], NN)


def left_part(momentum, gradient, right, opening, start, rows):
    n = momentum.shape[1]
    rank = right.shape[1]
    bm = tile(momentum.shape[0] // sum(SHARES))
    first = start // bm
    block = pl.BlockSpec((bm, n), lambda i: (i + first, 0))
    here = lambda i: (i, 0)
    out_specs = [pl.BlockSpec((bm, rank), here), pl.BlockSpec((bm, n), here)]
    out_shape = [jax.ShapeDtypeStruct((rows, rank), F32), pltpu.HBM((rows, n), F32)]
    if opening:
        out_specs.append(RESIDENT)
        out_shape.append(pltpu.VMEM((3 * n, rank), BF16))
        right, spec = in_hbm(right), pl.BlockSpec((n, rank), fixed)
    else:
        right, spec = near_core(right), RESIDENT
    return call(
        functools.partial(left_kernel, opening), 6 * rows * n * rank, rows * n * 6,
        grid=(rows // bm,),
        in_specs=[block, block, spec],
        out_specs=tuple(out_specs),
        out_shape=tuple(out_shape),
    )(in_hbm(momentum), in_hbm(gradient), right)


def cross_kernel(l_ref, c_ref, *refs):
    acc = refs[-1]
    n = c_ref.shape[1]
    left = along(l_ref[...].T, 1)
    step = min(n, 512)
    for c in range(0, n, step):
        value = dot(left, along_swapped(c_ref[:, c : c + step], 0), NN)
        acc[:, c : c + step] = value + refs[0][:, c : c + step] if len(refs) > 1 else value


def cross_part(left, combined, before):
    rows, rank = left.shape
    n = combined.shape[1]
    extra = [] if before is None else [before]
    return call(
        cross_kernel, 6 * rows * n * rank, rank * n * 8,
        in_specs=[RESIDENT] * (2 + len(extra)),
        out_specs=RESIDENT,
        out_shape=jax.ShapeDtypeStruct((rank, n), F32),
        input_output_aliases={2: 0} if extra else {},
    )(left, near_core(combined), *extra)


def gram_kernel(*refs):
    left = refs[0][...]
    value = dot(left, left, TN, HIGHEST)
    refs[-1][...] = value + refs[1][...] if len(refs) > 2 else value


def gram_part(left, before):
    rows, rank = left.shape
    extra = [] if before is None else [before]
    return call(
        gram_kernel, 12 * rows * rank * rank, rows * rank * 4,
        out_shape=jax.ShapeDtypeStruct((rank, rank), F32),
    )(left, *extra)


def inverse_kernel(g_ref, x_ref, work):
    rank = g_ref.shape[0]
    b = min(128, rank)
    rows = lax.broadcasted_iota(jnp.int32, (rank, rank), 0)
    cols = lax.broadcasted_iota(jnp.int32, (rank, rank), 1)
    work[:, :rank] = g_ref[...]
    work[:, rank:] = jnp.where(rows == cols, 1.0, 0.0).astype(F32)
    r = lax.broadcasted_iota(jnp.int32, (b, b), 0)
    c = lax.broadcasted_iota(jnp.int32, (b, b), 1)
    sub = lax.broadcasted_iota(jnp.int32, (b, 1), 0)
    for j in range(0, rank, b):
        unit = jnp.where(r == c, 1.0, 0.0).astype(F32)
        both = jnp.concatenate([work[j : j + b, j : j + b], unit], axis=1)
        for i in range(b):
            top = i // 8 * 8
            pivot = jnp.broadcast_to(both[i : i + 1, i : i + 1], (1, 2 * b))
            row = both[i : i + 1, :] * (1.0 / pivot)
            below = both[top:, :]
            below = below - jnp.where(sub[top:] > i, below[:, i : i + 1], 0.0) * row
            both = jnp.concatenate([both[:top], below], axis=0) if top else below
        pivots = jnp.sum(jnp.where(r == c, both[:, :b], 0.0), axis=1, keepdims=True)
        inv = both[:, b:] * lax.rsqrt(pivots)
        done = j + b
        panel = dot(inv, work[j:done, : rank + done], NN, HIGHEST)
        work[j:done, : rank + done] = panel
        if done < rank:
            work[done:, : rank + done] -= dot(panel[:, done:rank], panel, TN, HIGHEST)
    x_ref[...] = work[:, rank:]


def inverse_factor(gram):
    rank = gram.shape[0]
    return call(
        inverse_kernel, 12 * rank**3 * 20, rank * rank * 8,
        out_shape=jax.ShapeDtypeStruct((rank, rank), F32),
        scratch_shapes=[pltpu.VMEM((rank, 2 * rank), F32)],
    )(gram)


def basis_kernel(l_ref, x_ref, o_ref):
    o_ref[...] = dot(l_ref[...], x_ref[...], NT, HIGHEST)


def basis(left, inverse):
    rows, rank = left.shape
    return call(
        basis_kernel, 12 * rows * rank * rank, rows * rank * 8,
        out_shape=jax.ShapeDtypeStruct((rows, rank), F32),
    )(left, inverse)


def right_kernel(x_ref, z_ref, o_ref, s_ref):
    value = dot(x_ref[...], z_ref[...], NN, HIGHEST)
    o_ref[...] = value
    s_ref[...] = jnp.broadcast_to(jnp.sum(value * value, axis=1, keepdims=True), s_ref.shape)


def right_side(inverse, cross):
    rank, n = cross.shape
    return call(
        right_kernel, 12 * n * rank * rank, n * rank * 8,
        out_shape=(jax.ShapeDtypeStruct((rank, n), F32), jax.ShapeDtypeStruct((rank, 128), F32)),
    )(inverse, cross)


def momentum_kernel(first, half_ref, l_ref, r_ref, m_ref, g_ref, *refs):
    o_ref, split = refs[-2:]
    i = pl.program_id(0)
    bm, width = o_ref.shape

    @pl.when(i == 0)
    def _():
        high, low = halves(r_ref[...])
        split[...] = jnp.concatenate([high, low], axis=0)

    left = l_ref[...].astype(BF16)
    update = dot(jnp.concatenate([left, left], axis=1), split[...], NN)
    here = (
        pl.ds(pl.multiple_of((i + first) * bm, bm), bm),
        pl.ds(pl.multiple_of(half_ref[0] * width, width), width),
    )
    o_ref[...] = (m_ref[here] + g_ref[here].astype(F32)) - 0.05 * update


def momentum_half(half, left, right, momentum, gradient, start, stop, before):
    rows, n = momentum.shape
    rank, width = right.shape
    bm = tile((stop - start))
    first = start // bm
    extra = [] if before is None else [before]
    return pl.pallas_call(
        functools.partial(momentum_kernel, first),
        name="momentum",
        cost_estimate=pl.CostEstimate(flops=4 * (stop - start) * width * rank, bytes_accessed=(stop - start) * width * 4, transcendentals=0),
        compiler_params=pltpu.CompilerParams(vmem_limit_bytes=8 << 20),
        grid_spec=pltpu.PrefetchScalarGridSpec(
            num_scalar_prefetch=1,
            grid=((stop - start) // bm,),
            in_specs=[
                pl.BlockSpec((bm, rank), lambda i, half: (i + first, 0)),
                pl.BlockSpec((rank, width), lambda i, half: (0, 0)),
                RESIDENT,
                RESIDENT,
            ] + [pl.BlockSpec(memory_space=pl.ANY)] * len(extra),
            out_specs=pl.BlockSpec((bm, width), lambda i, half: (i + first, half[0])),
            scratch_shapes=[pltpu.VMEM((2 * rank, width), BF16)],
        ),
        out_shape=jax.ShapeDtypeStruct((rows, n), F32),
        input_output_aliases={5: 0} if extra else {},
    )(half, left, right, near_core(momentum), near_core(gradient), *extra)


def weight_kernel(count, half_ref, l_ref, a_ref, b_ref, s_ref, w_ref, o_ref, f_ref, split):
    @pl.when(pl.program_id(0) == 0)
    def _():
        scale = jnp.sqrt(s_ref[:, :1] / count + 1e-06)
        width = a_ref.shape[1]
        for side, ref in ((half_ref[0], a_ref), (1 - half_ref[0], b_ref)):
            factor = ref[...] / scale
            start = pl.multiple_of(side * width, width)
            split[:, pl.ds(start, width)] = along_swapped(factor, 0)
            f_ref[pl.ds(start, width), :] = factor.T

    left = along(l_ref[...], 1)
    bm, n = o_ref.shape
    here = pl.ds(pl.multiple_of(pl.program_id(0) * bm, bm), bm)
    step = min(n, 512)
    for c in range(0, n, step):
        update = dot(left, split[:, c : c + step], NN)
        o_ref[:, c : c + step] = w_ref[here, c : c + step] - 0.5 * update


def weight_update(half, left, own, other, squares, weight, count):
    rows, n = weight.shape
    rank, width = own.shape
    bm = tile(rows, 512)
    row = lambda i, half: (i, 0)
    still = lambda i, half: (0, 0)
    return pl.pallas_call(
        functools.partial(weight_kernel, float(count)),
        name="weight",
        cost_estimate=pl.CostEstimate(flops=6 * rows * n * rank, bytes_accessed=rows * n * 8, transcendentals=0),
        compiler_params=pltpu.CompilerParams(vmem_limit_bytes=20 << 20),
        grid_spec=pltpu.PrefetchScalarGridSpec(
            num_scalar_prefetch=1,
            grid=(rows // bm,),
            in_specs=[
                pl.BlockSpec((bm, rank), row),
                pl.BlockSpec((rank, width), still),
                pl.BlockSpec((rank, width), still),
                pl.BlockSpec(squares.shape, still),
                RESIDENT,
            ],
            out_specs=(pl.BlockSpec((bm, n), row), pl.BlockSpec((n, rank), still)),
            scratch_shapes=[pltpu.VMEM((3 * rank, n), BF16)],
        ),
        out_shape=(jax.ShapeDtypeStruct((rows, n), F32), jax.ShapeDtypeStruct((n, rank), F32)),
    )(half, left, own, other, squares, near_core(weight))


SHARES = (2, 2, 2, 2)


class Axis:
    def __init__(self, mesh, name):
        self.name, self.size = name, mesh.shape[name]
        self.bits = self.size.bit_length() - 1

    def swap(self, value, bit):
        return lax.ppermute(value, self.name, [(i, i ^ (1 << bit)) for i in range(self.size)])

    def place(self, bit):
        return (lax.axis_index(self.name) >> bit) & 1

    def exchange(self, value, bit):
        return value + self.swap(value, bit)

    def scatter(self, value, bit, dim=0):
        half = value.shape[dim] // 2
        here = self.place(bit)
        keep = lax.dynamic_slice_in_dim(value, here * half, half, dim)
        return keep + self.swap(lax.dynamic_slice_in_dim(value, (1 - here) * half, half, dim), bit)

    def gather(self, value, bit):
        other = self.swap(value, bit)
        first = jnp.concatenate([value, other])
        return jnp.where(self.place(bit) == 0, first, jnp.concatenate([other, value]))

    def total(self, value, bits):
        for bit in bits[:-1]:
            value = self.scatter(value, bit)
        value = self.exchange(value, bits[-1])
        for bit in bits[-2::-1]:
            value = self.gather(value, bit)
        return value


def on_device(col, row, weight, momentum, gradient, right_factor):
    rows, n = momentum.shape
    count = n * col.size
    near = col.bits // 2
    order = tuple(range(col.bits))
    orders = (order, order[near:] + order[:near] if near == 0 else (near,) + tuple(b for b in order if b != near))
    parts = len(SHARES)
    sizes = [share * rows // sum(SHARES) for share in SHARES]
    starts = [sum(sizes[:part]) for part in range(parts)]
    lefts, combined, cross, gram, right = [], [], None, None, right_factor
    for part in range(parts):
        got = left_part(momentum, gradient, right, part == 0, starts[part], sizes[part])
        right = got[2] if part == 0 else right
        combined.append(got[1])
        lefts.append(col.total(got[0], orders[part % 2]))
    for part in range(parts - 1):
        gram = gram_part(lefts[part], gram)
        cross = cross_part(lefts[part], combined[part], cross)
    gram = row.exchange(gram_part(lefts[-1], gram), 0)
    for bit in range(1, row.bits - 1):
        gram = row.exchange(gram, bit)
    last, gram = lax.optimization_barrier((lefts[-1], gram))
    other = row.swap(gram, row.bits - 1)
    cross = cross_part(last, combined[-1], cross)
    gram = gram + other
    half = row.place(0).astype(jnp.int32).reshape(1)
    cross = row.scatter(cross, 0, 1)
    for bit in range(1, row.bits - 1):
        cross = row.exchange(cross, bit)
    other = row.swap(cross, row.bits - 1)
    gram, _ = lax.optimization_barrier((gram, cross))
    inverse = inverse_factor(gram)
    left = basis(jnp.concatenate(lefts), inverse)
    own, squares = right_side(inverse, cross + other)
    other = row.swap(own, 0)
    squares = row.exchange(squares, 0)
    pieces = [(half, own, 0, rows), (1 - half, other, 0, rows // 2), (1 - half, other, rows // 2, rows)]
    new_momentum = None
    for bit in range(col.bits):
        squares = col.exchange(squares, bit)
        if bit < len(pieces):
            side, value, start, stop = pieces[bit]
            new_momentum = momentum_half(side, left, value, momentum, gradient, start, stop, new_momentum)
    new_weight, new_factor = weight_update(half, left, own, other, squares, weight, count)
    return new_weight, new_momentum, new_factor


def solution(mesh):
    col, row = Axis(mesh, "col"), Axis(mesh, "row")

    def body(*args):
        return on_device(col, row, *args)

    in_specs = (P("row", "col"), P("row", "col"), P("row", "col"), P("col", None))
    out_specs = (P("row", "col"), P("row", "col"), P("col", None))
    return jax.shard_map(body, mesh=mesh, in_specs=in_specs, out_specs=out_specs, check_vma=False)
```
